512 devices in a mesh: aux: 128 (over y, z, core), occ: 4 (over x).
Axes of the slice: x: 4, y: 8, z: 8, core: 2. Of those that a mesh axis runs over, the one named last changes fastest.
Arguments:
- factors: bfloat16 [256, 2048, 384], P('occ', 'aux'), may hold values from -0.5 to 0.5
- response: bfloat16 [256, 2048, 384], P('occ', 'aux'), may hold values from -0.5 to 0.5
- pattern: int32 [3, 3], replicated, may hold values 0 or 1
Outputs:
- exchange_k: float32 [384, 384], P('aux', 'occ')
The draws below stay inside these ranges and needn't reach their ends.
All inputs are finite; a program needn't handle non-finite values.
Results may differ from the reference program's by a relative error of at most 0.0003.
Values sent between devices are 32-bit elements; how exact they have to be, the bound alone decides.
A program may use at most 64 MiB of HBM per device.

```python
import jax
import jax.numpy as jnp
from jax import lax

NOCC = 256
BLK = 128
NBAS = 384
NAUX = 2048
NB = 3


def touch_ends(drawn, rng, least, largest):
    place = [jax.random.randint(jax.random.fold_in(rng, axis), (), 0, length) for axis, length in enumerate(drawn.shape)]
    longest = drawn.shape.index(max(drawn.shape))
    neighbour = place[:longest] + [(place[longest] + 1) % drawn.shape[longest]] + place[longest + 1:]
    return drawn.at[tuple(place)].set(least).at[tuple(neighbour)].set(largest)


def steps_of(own_key, extent, shards, least, high):
    level = 1.0
    for axis_at, parts in shards:
        draws = jax.random.uniform(jax.random.fold_in(jax.random.fold_in(own_key, 6), axis_at), (parts,), jnp.float32, least / len(shards), high / len(shards))
        level = level * jnp.repeat(jnp.exp(draws), extent[axis_at] // parts).reshape((-1,) + (1,) * (len(extent) - 1 - axis_at))
    return level


def bell_draw(stream_key, dims, deviation, most, pieces=(), held_as=jnp.bfloat16):
    factor_of = steps_of(stream_key, dims, pieces, -0.22, 0.18) if pieces else 1.0
    drawn = jax.random.normal(stream_key, dims, jnp.float32) * deviation * factor_of
    return jnp.minimum(jnp.maximum(drawn, -most), most).astype(held_as)


def setup_inputs(seed: int = 0) -> dict:
    arg_keys = jax.random.split(jax.random.key(seed), 4)
    return {
        "factors": bell_draw(arg_keys[0], (NOCC, NAUX, NBAS), ((NAUX * NOCC) ** -0.25), 0.5, ((0, 4), (1, 128))),
        "response": bell_draw(arg_keys[1], (NOCC, NAUX, NBAS), ((NAUX * NOCC) ** -0.25), 0.5, ((0, 4), (1, 128))),
        "pattern": touch_ends((jax.random.randint(arg_keys[2], (NB, NB), 0, 2) < 1).astype(jnp.int32), jax.random.fold_in(arg_keys[2], 1), 0, 1),
    }


def expand_tiles(pattern):
    tile_table = pattern.astype(jnp.float32)
    return jnp.repeat(jnp.repeat(tile_table, BLK, axis=0), BLK, axis=1)


def reference(factors, response, pattern):
    ground_rows = factors.reshape(NOCC * NAUX, NBAS)
    response_rows = response.reshape(NOCC * NAUX, NBAS)
    product = lax.dot_general(ground_rows, response_rows, (((0,), (0,)), ((), ())), preferred_element_type=jnp.float32)
    masked = expand_tiles(pattern) * product
    return 0.5 * (masked + masked.T)
```

```python
import jax
import jax.numpy as jnp
from jax import lax
from jax.experimental import pallas as pl
from jax.experimental.pallas import tpu as pltpu
from jax.sharding import PartitionSpec as P

X, Y, Z, C = 4, 8, 8, 2
SUB = 3
N = 384
COLS = N // X
F32 = jnp.float32
FAR8 = (4, 3, 5, 2, 6, 1, 7)
FAR4 = (2, 1, 3)


def kernel(
    a_hbm, b_hbm, p_hbm, o_ref,
    a_v, b_v, p_s, t_v,
    pair_src, pair_dst,
    x0_src, x0_dst, y0_src, y0_dst, z0_src, z0_dst,
    y1_src, y1_dst, z1_src, z1_dst, x1_src, x1_dst,
    z2_src, z2_dst, x2_src, x2_dst, y2_src, y2_dst,
    load_sem, pair_send, pair_recv, send4, recv4, send8, recv8,
):
    aux = lax.axis_index("aux")
    x = lax.axis_index("occ")
    c = lax.rem(aux, C)
    z = lax.rem(lax.div(aux, C), Z)
    y = lax.div(aux, C * Z)

    def at(x_, y_, z_, c_):
        return ((y_ * Z + z_) * C + c_, x_)

    def on_x(k):
        return at(lax.rem(x + k, X), y, z, c)

    def on_y(k):
        return at(x, lax.rem(y + k, Y), z, c)

    def on_z(k):
        return at(x, y, lax.rem(z + k, Z), c)

    partner = at(x, y, z, 1 - c)

    rows = a_v.shape[0]
    half = rows // 2
    loads = []
    for h in range(2):
        part = pl.ds(h * half, half)
        for n, (src, dst) in enumerate(((a_hbm, a_v), (b_hbm, b_v))):
            loads.append(pltpu.make_async_copy(src.at[part], dst.at[part], load_sem.at[2 * h + n]))
    p_load = pltpu.make_async_copy(p_hbm, p_s, load_sem.at[4])
    for ld in loads:
        ld.start()
    p_load.start()

    barrier = pltpu.get_barrier_semaphore()
    greeted = [partner]
    greeted += [on_y(k) for k in FAR8] + [on_z(k) for k in FAR8] + [on_x(k) for k in FAR4]
    for who in greeted:
        pl.semaphore_signal(barrier, inc=1, device_id=who, device_id_type=pl.DeviceIdType.MESH)

    def dot_t(l, r):
        return lax.dot_general(l, r, (((0,), (0,)), ((), ())), preferred_element_type=F32)

    loads[0].wait()
    loads[1].wait()
    s = dot_t(a_v[:half], b_v[:half])
    loads[2].wait()
    loads[3].wait()
    s = s + dot_t(a_v[half:], b_v[half:])
    p_load.wait()
    nb = p_s.shape[0]
    blk = N // nb
    for i in range(nb):
        for j in range(nb):
            f_ij = 0.5 * p_s[i, j].astype(F32)
            f_ji = 0.5 * p_s[j, i].astype(F32)
            r_i, r_j = slice(i * blk, (i + 1) * blk), slice(j * blk, (j + 1) * blk)
            t_v[j, r_i, :] = f_ij * s[r_i, r_j] + f_ji * s[r_j, r_i].T

    def pack(i):
        for cc in range(C):
            for j in range(nb):
                lanes = slice(j * blk, (j + 1) * blk)
                if i == 2:
                    for zz in range(Z):
                        got = t_v[j, pl.ds(6 * zz + 3 * cc + i, 8, stride=48), :]
                        pair_src[i, cc, 8 * zz:8 * zz + 8, lanes] = got
                else:
                    pair_src[i, cc, :, lanes] = t_v[j, pl.ds(3 * cc + i, 64, stride=6), :]

    def remote(src, dst, ss, rs, who):
        return pltpu.make_async_remote_copy(
            src_ref=src, dst_ref=dst, send_sem=ss, recv_sem=rs,
            device_id=who, device_id_type=pl.DeviceIdType.MESH,
        )

    pair = {}
    pl.semaphore_wait(barrier, len(greeted))
    for i in (2, 1, 0):
        pack(i)
        pair[i] = remote(
            pair_src.at[i, 1 - c], pair_dst.at[i], pair_send.at[i], pair_recv.at[i], partner
        )
        pair[i].start()

    sent = []

    def ring8(slot, to, me, src, dst):
        out = {}
        for k in FAR8:
            cp = remote(
                src.at[lax.rem(me + k, 8)], dst.at[k - 1],
                send8.at[slot, k - 1], recv8.at[slot, k - 1], to(k),
            )
            cp.start()
            out[k] = cp
        sent.extend(out.values())
        return out

    def ring4(slot, src, dst):
        out = {}
        for k in FAR4:
            cp = remote(
                src(lax.rem(x + k, X)), dst.at[k - 1],
                send4.at[slot, k - 1], recv4.at[slot, k - 1], on_x(k),
            )
            cp.start()
            out[k] = cp
        sent.extend(out.values())
        return out

    def total(own, copies, dst):
        acc = own
        for k in sorted(copies, key=lambda n: min(n, len(copies) + 1 - n)):
            copies[k].wait_recv()
            acc = acc + dst[k - 1]
        return acc

    def quarter(v, xx):
        return pltpu.roll(v, (N - COLS * xx) % N, 1)[:, :128] if xx else v[:, :128]

    pair[2].wait_recv()
    z2_src[...] = (pair_src[2, c] + pair_dst[2]).reshape(8, 8, N)
    z2 = ring8(0, on_z, z, z2_src, z2_dst)
    pair[1].wait_recv()
    y1_src[...] = (pair_src[1, c] + pair_dst[1]).reshape(8, 8, N)
    y1 = ring8(1, on_y, y, y1_src, y1_dst)
    pair[0].wait_recv()
    v = pair_src[0, c] + pair_dst[0]
    for xx in range(X):
        x0_src[xx] = quarter(v, xx)
    x0 = ring4(0, lambda t: x0_src.at[t], x0_dst)

    y0_src[...] = total(x0_src[x], x0, x0_dst).reshape(8, 8, 128)
    y0 = ring8(2, on_y, y, y0_src, y0_dst)
    v = total(y1_src[y], y1, y1_dst)
    for k in range(8):
        z1_src[k] = v[k:k + 1, :]
    z1 = ring8(3, on_z, z, z1_src, z1_dst)
    v = total(z2_src[z], z2, z2_dst)
    for xx in range(X):
        x2_src[xx] = quarter(v, xx)
    x2 = ring4(1, lambda t: x2_src.at[t], x2_dst)

    v = total(y0_src[y], y0, y0_dst)
    for k in range(8):
        z0_src[k] = v[k:k + 1, :]
    z0 = ring8(4, on_z, z, z0_src, z0_dst)
    v = total(x2_src[x], x2, x2_dst)
    for k in range(8):
        y2_src[k] = v[k:k + 1, :]
    y2 = ring8(5, on_y, y, y2_src, y2_dst)
    x1_src[...] = total(z1_src[z], z1, z1_dst)
    x1 = ring4(2, lambda t: x1_src, x1_dst)

    v = total(z0_src[z], z0, z0_dst)
    o_ref[0:1, :] = v[:, :COLS]
    v = total(y2_src[y], y2, y2_dst)
    o_ref[2:3, :] = v[:, :COLS]
    v = total(x1_src[...], x1, x1_dst)
    pick = quarter(v, 0)
    for xx in range(1, X):
        pick = jnp.where(x == xx, quarter(v, xx), pick)
    o_ref[1:2, :] = pick[:, :COLS]

    for i in range(SUB):
        pair[i].wait_send()
    for cp in sent:
        cp.wait_send()


def shards(factors, response, pattern):
    nocc_dev, aux_dev, nbasis = factors.shape
    rows = nocc_dev * aux_dev
    vm = pltpu.VMEM
    bf = factors.dtype
    scratch = [
        vm((rows, nbasis), bf), vm((rows, nbasis), bf), pltpu.SMEM(pattern.shape, jnp.int32),
        vm((pattern.shape[0], N, N // pattern.shape[0]), F32),
        vm((SUB, C, 64, N), F32), vm((SUB, 64, N), F32),
        vm((X, 64, 128), F32), vm((3, 64, 128), F32),
        vm((8, 8, 128), F32), vm((7, 8, 128), F32),
        vm((8, 1, 128), F32), vm((7, 1, 128), F32),
        vm((8, 8, N), F32), vm((7, 8, N), F32),
        vm((8, 1, N), F32), vm((7, 1, N), F32),
        vm((1, N), F32), vm((3, 1, N), F32),
        vm((8, 8, N), F32), vm((7, 8, N), F32),
        vm((X, 8, 128), F32), vm((3, 8, 128), F32),
        vm((8, 1, 128), F32), vm((7, 1, 128), F32),
        pltpu.SemaphoreType.DMA((5,)),
        pltpu.SemaphoreType.DMA((SUB,)), pltpu.SemaphoreType.DMA((SUB,)),
        pltpu.SemaphoreType.DMA((3, 3)), pltpu.SemaphoreType.DMA((3, 3)),
        pltpu.SemaphoreType.DMA((6, 7)), pltpu.SemaphoreType.DMA((6, 7)),
    ]
    return pl.pallas_call(
        kernel,
        out_shape=jax.ShapeDtypeStruct((SUB, COLS), F32),
        in_specs=[pl.BlockSpec(memory_space=pl.ANY)] * 3,
        out_specs=pl.BlockSpec(memory_space=pltpu.VMEM),
        scratch_shapes=scratch,
        compiler_params=pltpu.CompilerParams(collective_id=0, has_side_effects=True),
        name="exchange",
    )(factors.reshape(rows, nbasis), response.reshape(rows, nbasis), pattern)


def solution(mesh):
    in_specs = (P("occ", "aux", None), P("occ", "aux", None), P())
    out_specs = P("aux", "occ")
    return jax.shard_map(shards, mesh=mesh, in_specs=in_specs, out_specs=out_specs, check_vma=False)
```

```python
import jax
import jax.numpy as jnp
from jax import lax
from jax.experimental import pallas as pl
from jax.experimental.pallas import tpu as pltpu
from jax.sharding import PartitionSpec as P

X, Y, Z, C = 4, 8, 8, 2
SUB = 3
N = 384
COLS = N // X
F32 = jnp.float32
FAR8 = (4, 3, 5, 2, 6, 1, 7)
FAR4 = (2, 1, 3)


def kernel(
    a_hbm, b_hbm, p_hbm, o_ref,
    a_v, b_v, p_s, t_v,
    pair_src, pair_dst,
    x0_src, x0_dst, y0_src, y0_dst, z0_src, z0_dst,
    y1_src, y1_dst, z1_src, z1_dst, x1_src, x1_dst,
    z2_src, z2_dst, x2_src, x2_dst, y2_src, y2_dst,
    load_sem, pair_send, pair_recv, send4, recv4, send8, recv8,
):
    aux = lax.axis_index("aux")
    x = lax.axis_index("occ")
    c = lax.rem(aux, C)
    z = lax.rem(lax.div(aux, C), Z)
    y = lax.div(aux, C * Z)

    def at(x_, y_, z_, c_):
        return ((y_ * Z + z_) * C + c_, x_)

    def on_x(k):
        return at(lax.rem(x + k, X), y, z, c)

    def on_y(k):
        return at(x, lax.rem(y + k, Y), z, c)

    def on_z(k):
        return at(x, y, lax.rem(z + k, Z), c)

    partner = at(x, y, z, 1 - c)

    rows = a_v.shape[0]
    half = rows // 2
    loads = []
    for h in range(2):
        part = pl.ds(h * half, half)
        for n, (src, dst) in enumerate(((a_hbm, a_v), (b_hbm, b_v))):
            loads.append(pltpu.make_async_copy(src.at[part], dst.at[part], load_sem.at[2 * h + n]))
    p_load = pltpu.make_async_copy(p_hbm, p_s, load_sem.at[4])
    for ld in loads:
        ld.start()
    p_load.start()

    barrier = pltpu.get_barrier_semaphore()
    greeted = [partner]
    greeted += [on_y(k) for k in FAR8] + [on_z(k) for k in FAR8] + [on_x(k) for k in FAR4]
    for who in greeted:
        pl.semaphore_signal(barrier, inc=1, device_id=who, device_id_type=pl.DeviceIdType.MESH)

    def dot_t(l, r):
        return lax.dot_general(l, r, (((0,), (0,)), ((), ())), preferred_element_type=F32)

    loads[0].wait()
    loads[1].wait()
    s = dot_t(a_v[:half], b_v[:half])
    loads[2].wait()
    loads[3].wait()
    s = s + dot_t(a_v[half:], b_v[half:])
    p_load.wait()
    nb = p_s.shape[0]
    blk = N // nb
    for i in range(nb):
        for j in range(nb):
            f_ij = 0.5 * p_s[i, j].astype(F32)
            f_ji = 0.5 * p_s[j, i].astype(F32)
            r_i, r_j = slice(i * blk, (i + 1) * blk), slice(j * blk, (j + 1) * blk)
            t_v[j, r_i, :] = f_ij * s[r_i, r_j] + f_ji * s[r_j, r_i].T

    def pack(i):
        for cc in range(C):
            for j in range(nb):
                lanes = slice(j * blk, (j + 1) * blk)
                if i == 2:
                    for zz in range(Z):
                        got = t_v[j, pl.ds(6 * zz + 3 * cc + i, 8, stride=48), :]
                        pair_src[i, cc, 8 * zz:8 * zz + 8, lanes] = got
                else:
                    pair_src[i, cc, :, lanes] = t_v[j, pl.ds(3 * cc + i, 64, stride=6), :]

    def remote(src, dst, ss, rs, who):
        return pltpu.make_async_remote_copy(
            src_ref=src, dst_ref=dst, send_sem=ss, recv_sem=rs,
            device_id=who, device_id_type=pl.DeviceIdType.MESH,
        )

    pair = {}
    pl.semaphore_wait(barrier, len(greeted))
    for i in (2, 1, 0):
        pack(i)
        pair[i] = remote(
            pair_src.at[i, 1 - c], pair_dst.at[i], pair_send.at[i], pair_recv.at[i], partner
        )
        pair[i].start()

    sent = []

    def ring8(slot, to, me, src, dst):
        out = {}
        for k in FAR8:
            cp = remote(
                src.at[lax.rem(me + k, 8)], dst.at[k - 1],
                send8.at[slot, k - 1], recv8.at[slot, k - 1], to(k),
            )
            cp.start()
            out[k] = cp
        sent.extend(out.values())
        return out

    def ring4(slot, src, dst):
        out = {}
        for k in FAR4:
            cp = remote(
                src(lax.rem(x + k, X)), dst.at[k - 1],
                send4.at[slot, k - 1], recv4.at[slot, k - 1], on_x(k),
            )
            cp.start()
            out[k] = cp
        sent.extend(out.values())
        return out

    def total(own, copies, dst):
        acc = own
        for k in sorted(copies, key=lambda n: min(n, len(copies) + 1 - n)):
            copies[k].wait_recv()
            acc = acc + dst[k - 1]
        return acc

    def quarter(v, xx):
        return pltpu.roll(v, (N - COLS * xx) % N, 1)[:, :128] if xx else v[:, :128]

    pair[2].wait_recv()
    z2_src[...] = (pair_src[2, c] + pair_dst[2]).reshape(8, 8, N)
    z2 = ring8(0, on_z, z, z2_src, z2_dst)
    pair[1].wait_recv()
    y1_src[...] = (pair_src[1, c] + pair_dst[1]).reshape(8, 8, N)
    y1 = ring8(1, on_y, y, y1_src, y1_dst)
    pair[0].wait_recv()
    v = pair_src[0, c] + pair_dst[0]
    for xx in range(X):
        x0_src[xx] = quarter(v, xx)
    x0 = ring4(0, lambda t: x0_src.at[t], x0_dst)

    y0_src[...] = total(x0_src[x], x0, x0_dst).reshape(8, 8, 128)
    y0 = ring8(2, on_y, y, y0_src, y0_dst)
    v = total(y1_src[y], y1, y1_dst)
    for k in range(8):
        z1_src[k] = v[k:k + 1, :]
    z1 = ring8(3, on_z, z, z1_src, z1_dst)
    v = total(z2_src[z], z2, z2_dst)
    for xx in range(X):
        x2_src[xx] = quarter(v, xx)
    x2 = ring4(1, lambda t: x2_src.at[t], x2_dst)

    v = total(y0_src[y], y0, y0_dst)
    for k in range(8):
        z0_src[k] = v[k:k + 1, :]
    z0 = ring8(4, on_z, z, z0_src, z0_dst)
    v = total(x2_src[x], x2, x2_dst)
    for k in range(8):
        y2_src[k] = v[k:k + 1, :]
    y2 = ring8(5, on_y, y, y2_src, y2_dst)
    x1_src[...] = total(z1_src[z], z1, z1_dst)
    x1 = ring4(2, lambda t: x1_src, x1_dst)

    v = total(z0_src[z], z0, z0_dst)
    o_ref[0:1, :] = v[:, :COLS]
    v = total(y2_src[y], y2, y2_dst)
    o_ref[2:3, :] = v[:, :COLS]
    v = total(x1_src[...], x1, x1_dst)
    pick = quarter(v, 0)
    for xx in range(1, X):
        pick = jnp.where(x == xx, quarter(v, xx), pick)
    o_ref[1:2, :] = pick[:, :COLS]

    for i in range(SUB):
        pair[i].wait_send()
    for cp in sent:
        cp.wait_send()


def shards(factors, response, pattern):
    nocc_dev, aux_dev, nbasis = factors.shape
    rows = nocc_dev * aux_dev
    vm = pltpu.VMEM
    bf = factors.dtype
    scratch = [
        vm((rows, nbasis), bf), vm((rows, nbasis), bf), pltpu.SMEM(pattern.shape, jnp.int32),
        vm((pattern.shape[0], N, N // pattern.shape[0]), F32),
        vm((SUB, C, 64, N), F32), vm((SUB, 64, N), F32),
        vm((X, 64, 128), F32), vm((3, 64, 128), F32),
        vm((8, 8, 128), F32), vm((7, 8, 128), F32),
        vm((8, 1, 128), F32), vm((7, 1, 128), F32),
        vm((8, 8, N), F32), vm((7, 8, N), F32),
        vm((8, 1, N), F32), vm((7, 1, N), F32),
        vm((1, N), F32), vm((3, 1, N), F32),
        vm((8, 8, N), F32), vm((7, 8, N), F32),
        vm((X, 8, 128), F32), vm((3, 8, 128), F32),
        vm((8, 1, 128), F32), vm((7, 1, 128), F32),
        pltpu.SemaphoreType.DMA((5,)),
        pltpu.SemaphoreType.DMA((SUB,)), pltpu.SemaphoreType.DMA((SUB,)),
        pltpu.SemaphoreType.DMA((3, 3)), pltpu.SemaphoreType.DMA((3, 3)),
        pltpu.SemaphoreType.DMA((6, 7)), pltpu.SemaphoreType.DMA((6, 7)),
    ]
    return pl.pallas_call(
        kernel,
        out_shape=pltpu.VMEM((SUB, COLS), F32),
        in_specs=[pl.BlockSpec(memory_space=pl.ANY)] * 3,
        out_specs=pl.BlockSpec(memory_space=pltpu.VMEM),
        scratch_shapes=scratch,
        compiler_params=pltpu.CompilerParams(collective_id=0, has_side_effects=True),
        name="exchange",
    )(factors.reshape(rows, nbasis), response.reshape(rows, nbasis), pattern)


def solution(mesh):
    in_specs = (P("occ", "aux", None), P("occ", "aux", None), P())
    out_specs = P("aux", "occ")
    return jax.shard_map(shards, mesh=mesh, in_specs=in_specs, out_specs=out_specs, check_vma=False)
```

```python
import jax
import jax.numpy as jnp
from jax import lax
from jax.experimental import pallas as pl
from jax.experimental.pallas import tpu as pltpu
from jax.sharding import PartitionSpec as P

X, Y, Z, C = 4, 8, 8, 2
SUB = 3
N = 384
COLS = N // X
F32 = jnp.float32
FAR8 = (4, 3, 5, 2, 6, 1, 7)
FAR4 = (2, 1, 3)


def plane(n, m):
    steps = [(j, k) for j in range(n) for k in range(m) if j or k]
    return sorted(steps, key=lambda s: (-min(s[0], n - s[0]) - min(s[1], m - s[1]), s))


def kernel(
    a_hbm, b_hbm, p_hbm, o_ref,
    a_v, b_v, p_s, t_v,
    pair_src, pair_dst,
    x0_src, x0_dst, y1_src, y1_dst, z2_src, z2_dst,
    p0_src, p0_dst, p1_src, p1_dst, p2_src, p2_dst,
    load_sem, pair_send, pair_recv, send4, recv4, send8, recv8, plane_send, plane_recv, hello,
):
    aux = lax.axis_index("aux")
    x = lax.axis_index("occ")
    c = lax.rem(aux, C)
    z = lax.rem(lax.div(aux, C), Z)
    y = lax.div(aux, C * Z)

    def at(x_, y_, z_, c_):
        return ((y_ * Z + z_) * C + c_, x_)

    xs = [x if k == 0 else lax.rem(x + k, X) for k in range(X)]
    ys = [y if k == 0 else lax.rem(y + k, Y) for k in range(Y)]
    zs = [z if k == 0 else lax.rem(z + k, Z) for k in range(Z)]

    def on_x(k):
        return at(xs[k], y, z, c)

    def on_y(k):
        return at(x, ys[k], z, c)

    def on_z(k):
        return at(x, y, zs[k], c)

    partner = at(x, y, z, 1 - c)

    rows = a_v.shape[0]
    half = rows // 2
    loads = []
    for h in range(2):
        part = pl.ds(h * half, half)
        for n, (src, dst) in enumerate(((a_hbm, a_v), (b_hbm, b_v))):
            loads.append(pltpu.make_async_copy(src.at[part], dst.at[part], load_sem.at[2 * h + n]))
    p_load = pltpu.make_async_copy(p_hbm, p_s, load_sem.at[4])
    for ld in loads:
        ld.start()
    p_load.start()

    barrier = pltpu.get_barrier_semaphore()
    greeted = [partner]
    greeted += [on_y(k) for k in FAR8] + [on_z(k) for k in FAR8] + [on_x(k) for k in FAR4]
    for who in greeted:
        pl.semaphore_signal(barrier, inc=1, device_id=who, device_id_type=pl.DeviceIdType.MESH)

    def dot_t(l, r):
        return lax.dot_general(l, r, (((0,), (0,)), ((), ())), preferred_element_type=F32)

    loads[0].wait()
    loads[1].wait()
    s = dot_t(a_v[:half], b_v[:half])
    loads[2].wait()
    loads[3].wait()
    s = s + dot_t(a_v[half:], b_v[half:])
    p_load.wait()
    nb = p_s.shape[0]
    blk = N // nb
    for i in range(nb):
        for j in range(nb):
            f_ij = 0.5 * p_s[i, j].astype(F32)
            f_ji = 0.5 * p_s[j, i].astype(F32)
            r_i, r_j = slice(i * blk, (i + 1) * blk), slice(j * blk, (j + 1) * blk)
            t_v[j, r_i, :] = f_ij * s[r_i, r_j] + f_ji * s[r_j, r_i].T

    def pack(i):
        for cc in range(C):
            for j in range(nb):
                lanes = slice(j * blk, (j + 1) * blk)
                if i == 2:
                    for zz in range(Z):
                        got = t_v[j, pl.ds(6 * zz + 3 * cc + i, 8, stride=48), :]
                        pair_src[i, cc, 8 * zz:8 * zz + 8, lanes] = got
                else:
                    pair_src[i, cc, :, lanes] = t_v[j, pl.ds(3 * cc + i, 64, stride=6), :]

    def remote(src, dst, ss, rs, who):
        return pltpu.make_async_remote_copy(
            src_ref=src, dst_ref=dst, send_sem=ss, recv_sem=rs,
            device_id=who, device_id_type=pl.DeviceIdType.MESH,
        )

    pair = {}
    pl.semaphore_wait(barrier, len(greeted))
    for i in (2, 1, 0):
        pack(i)
        pair[i] = remote(
            pair_src.at[i, 1 - c], pair_dst.at[i], pair_send.at[i], pair_recv.at[i], partner
        )
        pair[i].start()

    for k in FAR8:
        pl.semaphore_signal(hello, inc=1, device_id=on_z(k), device_id_type=pl.DeviceIdType.MESH)

    sent = []

    def ring8(slot, to, steps, src, dst):
        out = {}
        for k in FAR8:
            cp = remote(
                src.at[steps[k]], dst.at[k - 1],
                send8.at[slot, k - 1], recv8.at[slot, k - 1], to(k),
            )
            cp.start()
            out[k] = cp
        sent.extend(out.values())
        return out

    def over_plane(slot, order, width, src, dst, pick, to):
        for j, k in order:
            remote(
                src.at[pick(j, k)], dst.at[j * width + k], plane_send.at[slot], plane_recv.at[slot], to(j, k)
            ).start()
        n = len(order)
        everything = remote(
            src.at[pl.ds(1, n)], dst.at[pl.ds(1, n)], plane_send.at[slot], plane_recv.at[slot], partner
        )
        sent.append(everything)
        return everything

    def total(own, copies, dst):
        acc = own
        for k in sorted(copies, key=lambda n: min(n, len(copies) + 1 - n)):
            copies[k].wait_recv()
            acc = acc + dst[k - 1]
        return acc

    def quarter(v, xx):
        return pltpu.roll(v, (N - COLS * xx) % N, 1)[:, :128] if xx else v[:, :128]

    pair[2].wait_recv()
    z2_src[...] = (pair_src[2, c] + pair_dst[2]).reshape(8, 8, N)
    z2 = ring8(0, on_z, zs, z2_src, z2_dst)
    pair[1].wait_recv()
    y1_src[...] = (pair_src[1, c] + pair_dst[1]).reshape(8, 8, N)
    y1 = ring8(1, on_y, ys, y1_src, y1_dst)
    pair[0].wait_recv()
    v = pair_src[0, c] + pair_dst[0]
    for xx in range(X):
        x0_src[xx] = quarter(v, xx)
    x0 = {}
    for k in FAR4:
        x0[k] = remote(x0_src.at[xs[k]], x0_dst.at[k - 1], send4.at[k - 1], recv4.at[k - 1], on_x(k))
        x0[k].start()
    sent.extend(x0.values())

    v = total(x0_src[x], x0, x0_dst)
    for r in range(Y * Z):
        p0_src[r] = v[r:r + 1, :]
    pl.semaphore_wait(hello, len(FAR8))
    p0 = over_plane(
        0, plane(Y, Z), Z, p0_src, p0_dst,
        lambda j, k: ys[j] * Z + zs[k], lambda j, k: at(x, ys[j], zs[k], c),
    )
    p0_dst[0] = p0_src[y * Z + z]

    v = total(z2_src[z], z2, z2_dst)
    for xx in range(X):
        q = quarter(v, xx)
        for r in range(Y):
            p2_src[xx * Y + r] = q[r:r + 1, :]
    p2 = over_plane(
        2, plane(X, Y), Y, p2_src, p2_dst,
        lambda j, k: xs[j] * Y + ys[k], lambda j, k: at(xs[j], ys[k], z, c),
    )
    p2_dst[0] = p2_src[x * Y + y]

    v = total(y1_src[y], y1, y1_dst)
    for xx in range(X):
        q = quarter(v, xx)
        for r in range(Z):
            p1_src[xx * Z + r] = q[r:r + 1, :]
    p1 = over_plane(
        1, plane(X, Z), Z, p1_src, p1_dst,
        lambda j, k: xs[j] * Z + zs[k], lambda j, k: at(xs[j], y, zs[k], c),
    )
    p1_dst[0] = p1_src[x * Z + z]

    for i, (cp, dst) in ((2, (p2, p2_dst)), (1, (p1, p1_dst)), (0, (p0, p0_dst))):
        cp.wait_recv()
        o_ref[i:i + 1, :] = jnp.sum(dst[...], axis=0)[:, :COLS]

    for i in range(SUB):
        pair[i].wait_send()
    for cp in sent:
        cp.wait_send()


def shards(factors, response, pattern):
    nocc_dev, aux_dev, nbasis = factors.shape
    rows = nocc_dev * aux_dev
    vm = pltpu.VMEM
    bf = factors.dtype
    scratch = [
        vm((rows, nbasis), bf), vm((rows, nbasis), bf), pltpu.SMEM(pattern.shape, jnp.int32),
        vm((pattern.shape[0], N, N // pattern.shape[0]), F32),
        vm((SUB, C, 64, N), F32), vm((SUB, 64, N), F32),
        vm((X, 64, 128), F32), vm((3, 64, 128), F32),
        vm((8, 8, N), F32), vm((7, 8, N), F32),
        vm((8, 8, N), F32), vm((7, 8, N), F32),
        vm((Y * Z, 1, 128), F32), vm((Y * Z, 1, 128), F32),
        vm((X * Z, 1, 128), F32), vm((X * Z, 1, 128), F32),
        vm((X * Y, 1, 128), F32), vm((X * Y, 1, 128), F32),
        pltpu.SemaphoreType.DMA((5,)),
        pltpu.SemaphoreType.DMA((SUB,)), pltpu.SemaphoreType.DMA((SUB,)),
        pltpu.SemaphoreType.DMA((3,)), pltpu.SemaphoreType.DMA((3,)),
        pltpu.SemaphoreType.DMA((2, 7)), pltpu.SemaphoreType.DMA((2, 7)),
        pltpu.SemaphoreType.DMA((3,)), pltpu.SemaphoreType.DMA((3,)),
        pltpu.SemaphoreType.REGULAR,
    ]
    return pl.pallas_call(
        kernel,
        out_shape=pltpu.VMEM((SUB, COLS), F32),
        in_specs=[pl.BlockSpec(memory_space=pl.ANY)] * 3,
        out_specs=pl.BlockSpec(memory_space=pltpu.VMEM),
        scratch_shapes=scratch,
        compiler_params=pltpu.CompilerParams(collective_id=0, has_side_effects=True),
        name="exchange",
    )(factors.reshape(rows, nbasis), response.reshape(rows, nbasis), pattern)


def solution(mesh):
    in_specs = (P("occ", "aux", None), P("occ", "aux", None), P())
    out_specs = P("aux", "occ")
    return jax.shard_map(shards, mesh=mesh, in_specs=in_specs, out_specs=out_specs, check_vma=False)
```

```python
import jax
import jax.numpy as jnp
from jax import lax
from jax.experimental import pallas as pl
from jax.experimental.pallas import tpu as pltpu
from jax.sharding import PartitionSpec as P

X, Y, Z, C = 4, 8, 8, 2
SUB = 3
N = 384
COLS = N // X
PARTS = 4
F32 = jnp.float32
FAR8 = (4, 3, 5, 2, 6, 1, 7)
FAR4 = (2, 1, 3)
NEAR8 = (2, 6, 1, 7)
VOUCH8 = (2, 6)


def plane(n, m):
    steps = [(j, k) for j in range(n) for k in range(m) if j or k]
    return sorted(steps, key=lambda s: (-min(s[0], n - s[0]) - min(s[1], m - s[1]), s))


def kernel(
    a_hbm, b_hbm, p_hbm, o_ref,
    a_v, b_v, p_s, t_v,
    pair_src, pair_dst,
    x0_src, x0_dst, y1_src, y1_dst, z2_src, z2_dst,
    p0_src, p0_dst, p1_src, p1_dst, p2_src, p2_dst,
    load_sem, pair_send, pair_recv, send4, recv4, send8, recv8, plane_send, plane_recv, vouch, hello,
):
    aux = lax.axis_index("aux")
    x = lax.axis_index("occ")
    c = lax.rem(aux, C)
    z = lax.rem(lax.div(aux, C), Z)
    y = lax.div(aux, C * Z)

    def at(x_, y_, z_, c_):
        return ((y_ * Z + z_) * C + c_, x_)

    xs = [x if k == 0 else lax.rem(x + k, X) for k in range(X)]
    ys = [y if k == 0 else lax.rem(y + k, Y) for k in range(Y)]
    zs = [z if k == 0 else lax.rem(z + k, Z) for k in range(Z)]

    def on_x(k):
        return at(xs[k], y, z, c)

    def on_y(k):
        return at(x, ys[k], z, c)

    def on_z(k):
        return at(x, y, zs[k], c)

    partner = at(x, y, z, 1 - c)

    rows = a_v.shape[0]
    part = rows // PARTS
    loads = []
    for h in range(PARTS):
        here = pl.ds(h * part, part)
        for n, (src, dst) in enumerate(((a_hbm, a_v), (b_hbm, b_v))):
            loads.append(pltpu.make_async_copy(src.at[here], dst.at[here], load_sem.at[2 * h + n]))
    p_load = pltpu.make_async_copy(p_hbm, p_s, load_sem.at[2 * PARTS])
    for ld in loads:
        ld.start()
    p_load.start()

    barrier = pltpu.get_barrier_semaphore()
    greeted = [partner]
    greeted += [on(k) for k in NEAR8 for on in (on_y, on_z)] + [on_x(k) for k in FAR4]
    for who in greeted:
        pl.semaphore_signal(barrier, inc=1, device_id=who, device_id_type=pl.DeviceIdType.MESH)

    def dot_t(l, r):
        return lax.dot_general(l, r, (((0,), (0,)), ((), ())), preferred_element_type=F32)

    s = 0.0
    for h in range(PARTS - 1):
        loads[2 * h].wait()
        loads[2 * h + 1].wait()
        s = s + dot_t(a_v[h * part:(h + 1) * part], b_v[h * part:(h + 1) * part])
    pl.semaphore_wait(barrier, len(greeted))
    vouchers = [on(k) for k in VOUCH8 for on in (on_y, on_z)]
    for who in vouchers:
        pl.semaphore_signal(vouch, inc=1, device_id=who, device_id_type=pl.DeviceIdType.MESH)
    loads[-2].wait()
    loads[-1].wait()
    s = s + dot_t(a_v[rows - part:], b_v[rows - part:])
    p_load.wait()
    nb = p_s.shape[0]
    blk = N // nb
    for i in range(nb):
        for j in range(nb):
            f_ij = 0.5 * p_s[i, j].astype(F32)
            f_ji = 0.5 * p_s[j, i].astype(F32)
            r_i, r_j = slice(i * blk, (i + 1) * blk), slice(j * blk, (j + 1) * blk)
            t_v[j, r_i, :] = f_ij * s[r_i, r_j] + f_ji * s[r_j, r_i].T

    def pack(i):
        for cc in range(C):
            for j in range(nb):
                lanes = slice(j * blk, (j + 1) * blk)
                if i == 2:
                    for zz in range(Z):
                        got = t_v[j, pl.ds(6 * zz + 3 * cc + i, 8, stride=48), :]
                        pair_src[i, cc, 8 * zz:8 * zz + 8, lanes] = got
                else:
                    pair_src[i, cc, :, lanes] = t_v[j, pl.ds(3 * cc + i, 64, stride=6), :]

    def remote(src, dst, ss, rs, who):
        return pltpu.make_async_remote_copy(
            src_ref=src, dst_ref=dst, send_sem=ss, recv_sem=rs,
            device_id=who, device_id_type=pl.DeviceIdType.MESH,
        )

    pair = {}
    for i in (2, 1, 0):
        pack(i)
        pair[i] = remote(
            pair_src.at[i, 1 - c], pair_dst.at[i], pair_send.at[i], pair_recv.at[i], partner
        )
        pair[i].start()

    sent = []

    def ring8(slot, to, steps, src, dst):
        out = {}
        for k in FAR8:
            cp = remote(
                src.at[steps[k]], dst.at[k - 1],
                send8.at[slot, k - 1], recv8.at[slot, k - 1], to(k),
            )
            cp.start()
            out[k] = cp
        sent.extend(out.values())
        return out

    def over_plane(slot, order, width, src, dst, pick, to):
        for j, k in order:
            remote(
                src.at[pick(j, k)], dst.at[j * width + k], plane_send.at[slot], plane_recv.at[slot], to(j, k)
            ).start()
        n = len(order)
        everything = remote(
            src.at[pl.ds(1, n)], dst.at[pl.ds(1, n)], plane_send.at[slot], plane_recv.at[slot], partner
        )
        sent.append(everything)
        return everything

    def total(own, copies, dst):
        acc = own
        for k in sorted(copies, key=lambda n: min(n, len(copies) + 1 - n)):
            copies[k].wait_recv()
            acc = acc + dst[k - 1]
        return acc

    def quarter(v, xx):
        return pltpu.roll(v, (N - COLS * xx) % N, 1)[:, :128] if xx else v[:, :128]

    pl.semaphore_wait(vouch, len(vouchers))
    pair[2].wait_recv()
    z2_src[...] = (pair_src[2, c] + pair_dst[2]).reshape(8, 8, N)
    z2 = ring8(0, on_z, zs, z2_src, z2_dst)
    pair[1].wait_recv()
    y1_src[...] = (pair_src[1, c] + pair_dst[1]).reshape(8, 8, N)
    y1 = ring8(1, on_y, ys, y1_src, y1_dst)
    pair[0].wait_recv()
    v = pair_src[0, c] + pair_dst[0]
    for xx in range(X):
        x0_src[xx] = quarter(v, xx)
    x0 = {}
    for k in FAR4:
        x0[k] = remote(x0_src.at[xs[k]], x0_dst.at[k - 1], send4.at[k - 1], recv4.at[k - 1], on_x(k))
        x0[k].start()
    sent.extend(x0.values())

    for k in FAR8:
        pl.semaphore_signal(hello, inc=1, device_id=on_z(k), device_id_type=pl.DeviceIdType.MESH)

    v = total(x0_src[x], x0, x0_dst)
    for r in range(Y * Z):
        p0_src[r] = v[r:r + 1, :]
    pl.semaphore_wait(hello, len(FAR8))
    p0 = over_plane(
        0, plane(Y, Z), Z, p0_src, p0_dst,
        lambda j, k: ys[j] * Z + zs[k], lambda j, k: at(x, ys[j], zs[k], c),
    )
    p0_dst[0] = p0_src[y * Z + z]

    v = total(z2_src[z], z2, z2_dst)
    for xx in range(X):
        q = quarter(v, xx)
        for r in range(Y):
            p2_src[xx * Y + r] = q[r:r + 1, :]
    p2 = over_plane(
        2, plane(X, Y), Y, p2_src, p2_dst,
        lambda j, k: xs[j] * Y + ys[k], lambda j, k: at(xs[j], ys[k], z, c),
    )
    p2_dst[0] = p2_src[x * Y + y]

    v = total(y1_src[y], y1, y1_dst)
    for xx in range(X):
        q = quarter(v, xx)
        for r in range(Z):
            p1_src[xx * Z + r] = q[r:r + 1, :]
    p1 = over_plane(
        1, plane(X, Z), Z, p1_src, p1_dst,
        lambda j, k: xs[j] * Z + zs[k], lambda j, k: at(xs[j], y, zs[k], c),
    )
    p1_dst[0] = p1_src[x * Z + z]

    for i, (cp, dst) in ((2, (p2, p2_dst)), (1, (p1, p1_dst)), (0, (p0, p0_dst))):
        cp.wait_recv()
        o_ref[i:i + 1, :] = jnp.sum(dst[...], axis=0)[:, :COLS]

    for i in range(SUB):
        pair[i].wait_send()
    for cp in sent:
        cp.wait_send()


def shards(factors, response, pattern):
    nocc_dev, aux_dev, nbasis = factors.shape
    rows = nocc_dev * aux_dev
    vm = pltpu.VMEM
    bf = factors.dtype
    scratch = [
        vm((rows, nbasis), bf), vm((rows, nbasis), bf), pltpu.SMEM(pattern.shape, jnp.int32),
        vm((pattern.shape[0], N, N // pattern.shape[0]), F32),
        vm((SUB, C, 64, N), F32), vm((SUB, 64, N), F32),
        vm((X, 64, 128), F32), vm((3, 64, 128), F32),
        vm((8, 8, N), F32), vm((7, 8, N), F32),
        vm((8, 8, N), F32), vm((7, 8, N), F32),
        vm((Y * Z, 1, 128), F32), vm((Y * Z, 1, 128), F32),
        vm((X * Z, 1, 128), F32), vm((X * Z, 1, 128), F32),
        vm((X * Y, 1, 128), F32), vm((X * Y, 1, 128), F32),
        pltpu.SemaphoreType.DMA((2 * PARTS + 1,)),
        pltpu.SemaphoreType.DMA((SUB,)), pltpu.SemaphoreType.DMA((SUB,)),
        pltpu.SemaphoreType.DMA((3,)), pltpu.SemaphoreType.DMA((3,)),
        pltpu.SemaphoreType.DMA((2, 7)), pltpu.SemaphoreType.DMA((2, 7)),
        pltpu.SemaphoreType.DMA((3,)), pltpu.SemaphoreType.DMA((3,)),
        pltpu.SemaphoreType.REGULAR, pltpu.SemaphoreType.REGULAR,
    ]
    return pl.pallas_call(
        kernel,
        out_shape=pltpu.VMEM((SUB, COLS), F32),
        in_specs=[pl.BlockSpec(memory_space=pl.ANY)] * 3,
        out_specs=pl.BlockSpec(memory_space=pltpu.VMEM),
        scratch_shapes=scratch,
        compiler_params=pltpu.CompilerParams(collective_id=0, has_side_effects=True),
        name="exchange",
    )(factors.reshape(rows, nbasis), response.reshape(rows, nbasis), pattern)


def solution(mesh):
    in_specs = (P("occ", "aux", None), P("occ", "aux", None), P())
    out_specs = P("aux", "occ")
    return jax.shard_map(shards, mesh=mesh, in_specs=in_specs, out_specs=out_specs, check_vma=False)
```

```python
import jax
import jax.numpy as jnp
from jax import lax
from jax.experimental import pallas as pl
from jax.experimental.pallas import tpu as pltpu
from jax.sharding import PartitionSpec as P

X, Y, Z, C = 4, 8, 8, 2
SUB = 3
N = 384
COLS = N // X
PARTS = 4
F32 = jnp.float32
FAR8 = (4, 3, 5, 2, 6, 1, 7)
FAR4 = (2, 1, 3)
NEAR8 = (2, 6, 1, 7)
VOUCH8 = (2, 6)
REST8 = (4, 3, 5)


def plane(n, m):
    steps = [(j, k) for j in range(n) for k in range(m) if j or k]
    return sorted(steps, key=lambda s: (-min(s[0], n - s[0]) - min(s[1], m - s[1]), s))


def kernel(
    a_hbm, b_hbm, p_hbm, o_ref,
    a_v, b_v, p_s, t_v,
    pair_src, pair_dst,
    x0_src, x0_dst, y1_src, y1_dst, z2_src, z2_dst,
    p0_src, p0_dst, p1_src, p1_dst, p2_src, p2_dst,
    load_sem, pair_send, pair_recv, send4, recv4, send8, recv8, plane_send, plane_recv, vouch, hello,
):
    aux = lax.axis_index("aux")
    x = lax.axis_index("occ")
    c = lax.rem(aux, C)
    z = lax.rem(lax.div(aux, C), Z)
    y = lax.div(aux, C * Z)

    def at(x_, y_, z_, c_):
        return ((y_ * Z + z_) * C + c_, x_)

    xs = [x if k == 0 else lax.rem(x + k, X) for k in range(X)]
    ys = [y if k == 0 else lax.rem(y + k, Y) for k in range(Y)]
    zs = [z if k == 0 else lax.rem(z + k, Z) for k in range(Z)]

    def on_x(k):
        return at(xs[k], y, z, c)

    def on_y(k):
        return at(x, ys[k], z, c)

    def on_z(k):
        return at(x, y, zs[k], c)

    partner = at(x, y, z, 1 - c)

    rows = a_v.shape[0]
    part = rows // PARTS
    loads = []
    for h in range(PARTS):
        here = pl.ds(h * part, part)
        for n, (src, dst) in enumerate(((a_hbm, a_v), (b_hbm, b_v))):
            loads.append(pltpu.make_async_copy(src.at[here], dst.at[here], load_sem.at[2 * h + n]))
    p_load = pltpu.make_async_copy(p_hbm, p_s, load_sem.at[2 * PARTS])
    for ld in loads:
        ld.start()
    p_load.start()

    barrier = pltpu.get_barrier_semaphore()
    greeted = [partner]
    greeted += [on(k) for k in NEAR8 for on in (on_z, on_y)] + [on_x(k) for k in FAR4]
    for who in greeted:
        pl.semaphore_signal(barrier, inc=1, device_id=who, device_id_type=pl.DeviceIdType.MESH)

    def dot_t(l, r):
        return lax.dot_general(l, r, (((0,), (0,)), ((), ())), preferred_element_type=F32)

    s = 0.0
    st = 0.0
    for h in range(PARTS - 1):
        loads[2 * h].wait()
        loads[2 * h + 1].wait()
        s = s + dot_t(a_v[h * part:(h + 1) * part], b_v[h * part:(h + 1) * part])
        st = st + dot_t(b_v[h * part:(h + 1) * part], a_v[h * part:(h + 1) * part])
    loads[-2].wait()
    loads[-1].wait()
    s = s + dot_t(a_v[rows - part:], b_v[rows - part:])
    st = st + dot_t(b_v[rows - part:], a_v[rows - part:])
    p_load.wait()
    nb = p_s.shape[0]
    blk = N // nb
    for i in range(nb):
        for j in range(nb):
            f_ij = 0.5 * p_s[i, j].astype(F32)
            f_ji = 0.5 * p_s[j, i].astype(F32)
            r_i, r_j = slice(i * blk, (i + 1) * blk), slice(j * blk, (j + 1) * blk)
            t_v[j, r_i, :] = f_ij * s[r_i, r_j] + f_ji * st[r_i, r_j]

    def pack(i):
        for cc in range(C):
            for j in range(nb):
                lanes = slice(j * blk, (j + 1) * blk)
                if i == 2:
                    for zz in range(Z):
                        got = t_v[j, pl.ds(6 * zz + 3 * cc + i, 8, stride=48), :]
                        pair_src[i, cc, 8 * zz:8 * zz + 8, lanes] = got
                else:
                    pair_src[i, cc, :, lanes] = t_v[j, pl.ds(3 * cc + i, 64, stride=6), :]

    def remote(src, dst, ss, rs, who):
        return pltpu.make_async_remote_copy(
            src_ref=src, dst_ref=dst, send_sem=ss, recv_sem=rs,
            device_id=who, device_id_type=pl.DeviceIdType.MESH,
        )

    pl.semaphore_wait(barrier, len(greeted))
    vouchers = [on(k) for k in VOUCH8 for on in (on_z, on_y)]
    for who in vouchers:
        pl.semaphore_signal(vouch, inc=1, device_id=who, device_id_type=pl.DeviceIdType.MESH)
    pair = {}
    for i in (2, 1, 0):
        pack(i)
        pair[i] = remote(
            pair_src.at[i, 1 - c], pair_dst.at[i], pair_send.at[i], pair_recv.at[i], partner
        )
        pair[i].start()

    sent = []

    def ring8(slot, to, steps, src, dst, some):
        out = {}
        for k in some:
            cp = remote(
                src.at[steps[k]], dst.at[k - 1],
                send8.at[slot, k - 1], recv8.at[slot, k - 1], to(k),
            )
            cp.start()
            out[k] = cp
        sent.extend(out.values())
        return out

    def over_plane(slot, order, width, src, dst, pick, to):
        for j, k in order:
            remote(
                src.at[pick(j, k)], dst.at[j * width + k], plane_send.at[slot], plane_recv.at[slot], to(j, k)
            ).start()
        n = len(order)
        everything = remote(
            src.at[pl.ds(1, n)], dst.at[pl.ds(1, n)], plane_send.at[slot], plane_recv.at[slot], partner
        )
        sent.append(everything)
        return everything

    def total(own, copies, dst):
        acc = own
        for k in sorted(copies, key=lambda n: min(n, len(copies) + 1 - n)):
            copies[k].wait_recv()
            acc = acc + dst[k - 1]
        return acc

    def quarter(v, xx):
        return pltpu.roll(v, (N - COLS * xx) % N, 1)[:, :128] if xx else v[:, :128]

    pair[2].wait_recv()
    z2_src[...] = (pair_src[2, c] + pair_dst[2]).reshape(8, 8, N)
    z2 = ring8(0, on_z, zs, z2_src, z2_dst, NEAR8)
    pl.semaphore_wait(vouch, len(vouchers))
    z2 |= ring8(0, on_z, zs, z2_src, z2_dst, REST8)
    pair[1].wait_recv()
    y1_src[...] = (pair_src[1, c] + pair_dst[1]).reshape(8, 8, N)
    y1 = ring8(1, on_y, ys, y1_src, y1_dst, FAR8)
    pair[0].wait_recv()
    v = pair_src[0, c] + pair_dst[0]
    for xx in range(X):
        x0_src[xx] = quarter(v, xx)
    x0 = {}
    for k in FAR4:
        x0[k] = remote(x0_src.at[xs[k]], x0_dst.at[k - 1], send4.at[k - 1], recv4.at[k - 1], on_x(k))
        x0[k].start()
    sent.extend(x0.values())

    for k in FAR8:
        pl.semaphore_signal(hello, inc=1, device_id=on_z(k), device_id_type=pl.DeviceIdType.MESH)

    v = total(x0_src[x], x0, x0_dst)
    for r in range(Y * Z):
        p0_src[r] = v[r:r + 1, :]
    pl.semaphore_wait(hello, len(FAR8))
    p0 = over_plane(
        0, plane(Y, Z), Z, p0_src, p0_dst,
        lambda j, k: ys[j] * Z + zs[k], lambda j, k: at(x, ys[j], zs[k], c),
    )
    p0_dst[0] = p0_src[y * Z + z]

    v = total(z2_src[z], z2, z2_dst)
    for xx in range(X):
        q = quarter(v, xx)
        for r in range(Y):
            p2_src[xx * Y + r] = q[r:r + 1, :]
    p2 = over_plane(
        2, plane(X, Y), Y, p2_src, p2_dst,
        lambda j, k: xs[j] * Y + ys[k], lambda j, k: at(xs[j], ys[k], z, c),
    )
    p2_dst[0] = p2_src[x * Y + y]

    v = total(y1_src[y], y1, y1_dst)
    for xx in range(X):
        q = quarter(v, xx)
        for r in range(Z):
            p1_src[xx * Z + r] = q[r:r + 1, :]
    p1 = over_plane(
        1, plane(X, Z), Z, p1_src, p1_dst,
        lambda j, k: xs[j] * Z + zs[k], lambda j, k: at(xs[j], y, zs[k], c),
    )
    p1_dst[0] = p1_src[x * Z + z]

    for i in range(SUB):
        pair[i].wait_send()
    for cp in sent:
        cp.wait_send()

    for i, (cp, dst) in ((2, (p2, p2_dst)), (1, (p1, p1_dst)), (0, (p0, p0_dst))):
        cp.wait_recv()
        o_ref[i:i + 1, :] = jnp.sum(dst[...], axis=0)[:, :COLS]


def shards(factors, response, pattern):
    nocc_dev, aux_dev, nbasis = factors.shape
    rows = nocc_dev * aux_dev
    vm = pltpu.VMEM
    bf = factors.dtype
    scratch = [
        vm((rows, nbasis), bf), vm((rows, nbasis), bf), pltpu.SMEM(pattern.shape, jnp.int32),
        vm((pattern.shape[0], N, N // pattern.shape[0]), F32),
        vm((SUB, C, 64, N), F32), vm((SUB, 64, N), F32),
        vm((X, 64, 128), F32), vm((3, 64, 128), F32),
        vm((8, 8, N), F32), vm((7, 8, N), F32),
        vm((8, 8, N), F32), vm((7, 8, N), F32),
        vm((Y * Z, 1, 128), F32), vm((Y * Z, 1, 128), F32),
        vm((X * Z, 1, 128), F32), vm((X * Z, 1, 128), F32),
        vm((X * Y, 1, 128), F32), vm((X * Y, 1, 128), F32),
        pltpu.SemaphoreType.DMA((2 * PARTS + 1,)),
        pltpu.SemaphoreType.DMA((SUB,)), pltpu.SemaphoreType.DMA((SUB,)),
        pltpu.SemaphoreType.DMA((3,)), pltpu.SemaphoreType.DMA((3,)),
        pltpu.SemaphoreType.DMA((2, 7)), pltpu.SemaphoreType.DMA((2, 7)),
        pltpu.SemaphoreType.DMA((3,)), pltpu.SemaphoreType.DMA((3,)),
        pltpu.SemaphoreType.REGULAR, pltpu.SemaphoreType.REGULAR,
    ]
    return pl.pallas_call(
        kernel,
        out_shape=pltpu.VMEM((SUB, COLS), F32),
        in_specs=[pl.BlockSpec(memory_space=pl.ANY)] * 3,
        out_specs=pl.BlockSpec(memory_space=pltpu.VMEM),
        scratch_shapes=scratch,
        compiler_params=pltpu.CompilerParams(collective_id=0, has_side_effects=True),
        name="exchange",
    )(factors.reshape(rows, nbasis), response.reshape(rows, nbasis), pattern)


def solution(mesh):
    in_specs = (P("occ", "aux", None), P("occ", "aux", None), P())
    out_specs = P("aux", "occ")
    return jax.shard_map(shards, mesh=mesh, in_specs=in_specs, out_specs=out_specs, check_vma=False)
```

```python
import jax
import jax.numpy as jnp
from jax import lax
from jax.experimental import pallas as pl
from jax.experimental.pallas import tpu as pltpu
from jax.sharding import PartitionSpec as P

X, Y, Z, C = 4, 8, 8, 2
SUB = 3
N = 384
COLS = N // X
PARTS = 4
F32 = jnp.float32
FAR8 = (4, 3, 5, 2, 6, 1, 7)
FAR4 = (2, 1, 3)
NEAR8 = (2, 6, 1, 7)
VOUCH8 = (2, 6)
REST8 = (4, 3, 5)


def plane(n, m):
    steps = [(j, k) for j in range(n) for k in range(m) if j or k]
    return sorted(steps, key=lambda s: (-min(s[0], n - s[0]) - min(s[1], m - s[1]), s))


def kernel(
    a_hbm, b_hbm, p_hbm, o_ref,
    a_v, b_v, p_s, t_v,
    pair_src, pair_dst,
    x0_src, x0_dst, y1_src, y1_dst, z2_src, z2_dst,
    p0_src, p0_dst, p1_src, p1_dst, p2_src, p2_dst,
    load_sem, pair_send, pair_recv, send4, recv4, send8, recv8, plane_send, plane_recv, vouch, hello,
):
    aux = lax.axis_index("aux")
    x = lax.axis_index("occ")
    c = lax.rem(aux, C)
    z = lax.rem(lax.div(aux, C), Z)
    y = lax.div(aux, C * Z)

    def at(x_, y_, z_, c_):
        return ((y_ * Z + z_) * C + c_, x_)

    xs = [x if k == 0 else lax.rem(x + k, X) for k in range(X)]
    ys = [y if k == 0 else lax.rem(y + k, Y) for k in range(Y)]
    zs = [z if k == 0 else lax.rem(z + k, Z) for k in range(Z)]

    def on_x(k):
        return at(xs[k], y, z, c)

    def on_y(k):
        return at(x, ys[k], z, c)

    def on_z(k):
        return at(x, y, zs[k], c)

    partner = at(x, y, z, 1 - c)

    rows = a_v.shape[0]
    part = rows // PARTS
    loads = []
    for h in range(PARTS):
        here = pl.ds(h * part, part)
        for n, (src, dst) in enumerate(((a_hbm, a_v), (b_hbm, b_v))):
            loads.append(pltpu.make_async_copy(src.at[here], dst.at[here], load_sem.at[2 * h + n]))
    p_load = pltpu.make_async_copy(p_hbm, p_s, load_sem.at[2 * PARTS])
    for ld in loads:
        ld.start()
    p_load.start()

    barrier = pltpu.get_barrier_semaphore()
    greeted = [partner]
    greeted += [on(k) for k in NEAR8 for on in (on_z, on_y)] + [on_x(k) for k in FAR4]
    for who in greeted:
        pl.semaphore_signal(barrier, inc=1, device_id=who, device_id_type=pl.DeviceIdType.MESH)

    def dot_t(l, r):
        return lax.dot_general(l, r, (((0,), (0,)), ((), ())), preferred_element_type=F32)

    s = 0.0
    st = 0.0
    for h in range(PARTS - 1):
        loads[2 * h].wait()
        loads[2 * h + 1].wait()
        s = s + dot_t(a_v[h * part:(h + 1) * part], b_v[h * part:(h + 1) * part])
        st = st + dot_t(b_v[h * part:(h + 1) * part], a_v[h * part:(h + 1) * part])
    loads[-2].wait()
    loads[-1].wait()
    s = s + dot_t(a_v[rows - part:], b_v[rows - part:])
    st = st + dot_t(b_v[rows - part:], a_v[rows - part:])
    p_load.wait()
    nb = p_s.shape[0]
    blk = N // nb
    for i in range(nb):
        for j in range(nb):
            f_ij = 0.5 * p_s[i, j].astype(F32)
            f_ji = 0.5 * p_s[j, i].astype(F32)
            r_i, r_j = slice(i * blk, (i + 1) * blk), slice(j * blk, (j + 1) * blk)
            t_v[j, r_i, :] = f_ij * s[r_i, r_j] + f_ji * st[r_i, r_j]

    def pack(i):
        for cc in range(C):
            for j in range(nb):
                lanes = slice(j * blk, (j + 1) * blk)
                if i == 2:
                    for zz in range(Z):
                        got = t_v[j, pl.ds(6 * zz + 3 * cc + i, 8, stride=48), :]
                        pair_src[i, cc, 8 * zz:8 * zz + 8, lanes] = got
                else:
                    pair_src[i, cc, :, lanes] = t_v[j, pl.ds(3 * cc + i, 64, stride=6), :]

    def remote(src, dst, ss, rs, who):
        return pltpu.make_async_remote_copy(
            src_ref=src, dst_ref=dst, send_sem=ss, recv_sem=rs,
            device_id=who, device_id_type=pl.DeviceIdType.MESH,
        )

    pl.semaphore_wait(barrier, len(greeted))
    vouchers = [on(k) for k in VOUCH8 for on in (on_z, on_y)]
    for who in vouchers:
        pl.semaphore_signal(vouch, inc=1, device_id=who, device_id_type=pl.DeviceIdType.MESH)
    pair = {}
    for i in (2, 1, 0):
        pack(i)
        pair[i] = remote(
            pair_src.at[i, 1 - c], pair_dst.at[i], pair_send.at[i], pair_recv.at[i], partner
        )
        pair[i].start()

    sent = []

    def ring8(slot, to, steps, src, dst, some):
        out = {}
        for k in some:
            cp = remote(
                src.at[steps[k]], dst.at[k - 1],
                send8.at[slot, k - 1], recv8.at[slot, k - 1], to(k),
            )
            cp.start()
            out[k] = cp
        sent.extend(out.values())
        return out

    def over_plane(slot, order, width, src, dst, pick, to):
        for j, k in order:
            remote(
                src.at[pick(j, k)], dst.at[j * width + k], plane_send.at[slot], plane_recv.at[slot], to(j, k)
            ).start()
        n = len(order)
        everything = remote(
            src.at[pl.ds(1, n)], dst.at[pl.ds(1, n)], plane_send.at[slot], plane_recv.at[slot], partner
        )
        sent.append(everything)
        return everything

    def total(own, copies, dst):
        acc = own
        for k in sorted(copies, key=lambda n: min(n, len(copies) + 1 - n)):
            copies[k].wait_recv()
            acc = acc + dst[k - 1]
        return acc

    def quarter(v, xx):
        return pltpu.roll(v, (N - COLS * xx) % N, 1)[:, :128] if xx else v[:, :128]

    pair[2].wait_recv()
    z2_src[...] = (pair_src[2, c] + pair_dst[2]).reshape(8, 8, N)
    z2 = ring8(0, on_z, zs, z2_src, z2_dst, NEAR8)
    pl.semaphore_wait(vouch, len(vouchers))
    z2 |= ring8(0, on_z, zs, z2_src, z2_dst, REST8)
    pair[1].wait_recv()
    y1_src[...] = (pair_src[1, c] + pair_dst[1]).reshape(8, 8, N)
    y1 = ring8(1, on_y, ys, y1_src, y1_dst, FAR8)
    for k in FAR8:
        pl.semaphore_signal(hello, inc=1, device_id=on_z(k), device_id_type=pl.DeviceIdType.MESH)

    pair[0].wait_recv()
    v = pair_src[0, c] + pair_dst[0]
    for xx in range(X):
        x0_src[xx] = quarter(v, xx)
    x0 = {}
    for k in FAR4:
        x0[k] = remote(x0_src.at[xs[k]], x0_dst.at[k - 1], send4.at[k - 1], recv4.at[k - 1], on_x(k))
        x0[k].start()
    sent.extend(x0.values())

    v = total(x0_src[x], x0, x0_dst)
    for r in range(Y * Z):
        p0_src[r] = v[r:r + 1, :]
    pl.semaphore_wait(hello, len(FAR8))
    p0 = over_plane(
        0, plane(Y, Z), Z, p0_src, p0_dst,
        lambda j, k: ys[j] * Z + zs[k], lambda j, k: at(x, ys[j], zs[k], c),
    )
    p0_dst[0] = p0_src[y * Z + z]

    v = total(z2_src[z], z2, z2_dst)
    for xx in range(X):
        q = quarter(v, xx)
        for r in range(Y):
            p2_src[xx * Y + r] = q[r:r + 1, :]
    p2 = over_plane(
        2, plane(X, Y), Y, p2_src, p2_dst,
        lambda j, k: xs[j] * Y + ys[k], lambda j, k: at(xs[j], ys[k], z, c),
    )
    p2_dst[0] = p2_src[x * Y + y]

    v = total(y1_src[y], y1, y1_dst)
    for xx in range(X):
        q = quarter(v, xx)
        for r in range(Z):
            p1_src[xx * Z + r] = q[r:r + 1, :]
    p1 = over_plane(
        1, plane(X, Z), Z, p1_src, p1_dst,
        lambda j, k: xs[j] * Z + zs[k], lambda j, k: at(xs[j], y, zs[k], c),
    )
    p1_dst[0] = p1_src[x * Z + z]

    for i in range(SUB):
        pair[i].wait_send()
    for cp in sent:
        cp.wait_send()

    for i, (cp, dst) in ((2, (p2, p2_dst)), (1, (p1, p1_dst)), (0, (p0, p0_dst))):
        cp.wait_recv()
        o_ref[i:i + 1, :] = jnp.sum(dst[...], axis=0)[:, :COLS]


def shards(factors, response, pattern):
    nocc_dev, aux_dev, nbasis = factors.shape
    rows = nocc_dev * aux_dev
    vm = pltpu.VMEM
    bf = factors.dtype
    scratch = [
        vm((rows, nbasis), bf), vm((rows, nbasis), bf), pltpu.SMEM(pattern.shape, jnp.int32),
        vm((pattern.shape[0], N, N // pattern.shape[0]), F32),
        vm((SUB, C, 64, N), F32), vm((SUB, 64, N), F32),
        vm((X, 64, 128), F32), vm((3, 64, 128), F32),
        vm((8, 8, N), F32), vm((7, 8, N), F32),
        vm((8, 8, N), F32), vm((7, 8, N), F32),
        vm((Y * Z, 1, 128), F32), vm((Y * Z, 1, 128), F32),
        vm((X * Z, 1, 128), F32), vm((X * Z, 1, 128), F32),
        vm((X * Y, 1, 128), F32), vm((X * Y, 1, 128), F32),
        pltpu.SemaphoreType.DMA((2 * PARTS + 1,)),
        pltpu.SemaphoreType.DMA((SUB,)), pltpu.SemaphoreType.DMA((SUB,)),
        pltpu.SemaphoreType.DMA((3,)), pltpu.SemaphoreType.DMA((3,)),
        pltpu.SemaphoreType.DMA((2, 7)), pltpu.SemaphoreType.DMA((2, 7)),
        pltpu.SemaphoreType.DMA((3,)), pltpu.SemaphoreType.DMA((3,)),
        pltpu.SemaphoreType.REGULAR, pltpu.SemaphoreType.REGULAR,
    ]
    return pl.pallas_call(
        kernel,
        out_shape=pltpu.VMEM((SUB, COLS), F32),
        in_specs=[pl.BlockSpec(memory_space=pl.ANY)] * 3,
        out_specs=pl.BlockSpec(memory_space=pltpu.VMEM),
        scratch_shapes=scratch,
        compiler_params=pltpu.CompilerParams(collective_id=0, has_side_effects=True),
        name="exchange",
    )(factors.reshape(rows, nbasis), response.reshape(rows, nbasis), pattern)


def solution(mesh):
    in_specs = (P("occ", "aux", None), P("occ", "aux", None), P())
    out_specs = P("aux", "occ")
    return jax.shard_map(shards, mesh=mesh, in_specs=in_specs, out_specs=out_specs, check_vma=False)
```
